32 devices in a mesh: blk: 8 (over y, x, core), fsdp: 4 (over z).
Axes of the slice: x: 2, y: 2, z: 4, core: 2. Of those that a mesh axis runs over, the one named last changes fastest.
Arguments:
- hidden: bfloat16 [8, 512, 5120], P('blk', 'fsdp'), may hold values from -6 to 6
- grad_query: bfloat16 [8, 512, 5120], P('blk', 'fsdp'), may hold values from -6 to 6
- grad_value: bfloat16 [8, 512, 5120], P('blk', 'fsdp'), may hold values from -6 to 6
- adapters: bfloat16 [8, 192, 5120], P('blk', 'fsdp'), may hold values from -4 to 4
- first_moment: bfloat16 [8, 192, 5120], P('blk', 'fsdp'), may hold values from -0.009765625 to 0.009765625
- second_moment: bfloat16 [8, 192, 5120], P('blk', 'fsdp'), may hold values from 8.090865e-09 to 8.1025064e-08
- mixing: int32 [8, 3], P('blk'), may hold values from 1 to 2, as said below
Outputs:
- mixed: bfloat16 [8, 192, 5120], P('blk', 'fsdp')
The draws below stay inside these ranges and needn't reach their ends.
Inputs may be any that keep to these rules, and one draw needn't show every extreme that they name: `mixing`: each row holds two numerators equal to 1 and one equal to 2.
All inputs are finite; a program needn't handle non-finite values.
Results may differ from the reference program's by a relative error of at most 0.0051.
Values may be sent and summed in bfloat16 or wider, within the bound.
A program may use at most 64 MiB of HBM per device.

```python
import math
import jax
import jax.numpy as jnp
from jax import lax

D = 5120
R = 48
TOK_DEV = 128
ROWS = 192
GROUPS = 8
TOKG = 512
N_FSDP = 4


def draw_mixing(key, part):
    position = jax.random.randint(key, (GROUPS, 1), 0, 3)
    columns = jnp.arange(3)[None, :]
    return (1 + (columns == position).astype(jnp.int32)).astype(jnp.int32)


def shard_levels(rng, shape, split, smallest, largest):
    level, own = 1.0, jax.random.fold_in(rng, 6)
    for dim, shards_of in split:
        draws = jnp.exp(jax.random.uniform(jax.random.fold_in(own, dim), (shards_of,), jnp.float32, smallest / len(split), largest / len(split)))
        level = level * jnp.repeat(draws, shape[dim] // shards_of).reshape([-1 if axis == dim else 1 for axis in range(len(shape))])
    return level


def scatter_about(rng, shape, deviation, most, split=(), kind=jnp.bfloat16):
    factor_of = shard_levels(rng, shape, split, -0.22, 0.18) if split else 1.0
    entries = jax.random.normal(rng, shape, jnp.float32) * deviation * factor_of
    return jnp.minimum(jnp.maximum(entries, -most), most).astype(kind)


def setup_inputs(seed: int = 0) -> dict:
    streams_of = jax.random.split(jax.random.key(seed), 8)
    return {
        "hidden": scatter_about(streams_of[0], (GROUPS, TOKG, D), 1.0, 6.0, ((0, 8), (1, 4))),
        "grad_query": scatter_about(streams_of[1], (GROUPS, TOKG, D), 1.0, 6.0, ((0, 8), (1, 4))),
        "grad_value": scatter_about(streams_of[2], (GROUPS, TOKG, D), 1.0, 6.0, ((0, 8), (1, 4))),
        "adapters": scatter_about(streams_of[3], (GROUPS, ROWS, D), 1.0, 4.0, ((0, 8), (1, 4))),
        "first_moment": scatter_about(streams_of[4], (GROUPS, ROWS, D), (0.1 / (TOKG * R) ** 0.5), 0.009765625, ((0, 8), (1, 4))),
        "second_moment": jnp.clip(jnp.exp(math.log(8.102506399154663e-08) - 2.3040229 * jax.random.uniform(streams_of[5], (GROUPS, ROWS, D), jnp.float32) ** shard_levels(streams_of[5], (GROUPS, ROWS, D), ((0, 8), (1, 4)), -0.2, 0.2)), 8.09086486697197e-09, 8.102506399154663e-08).astype(jnp.bfloat16),
        "mixing": draw_mixing(jax.random.fold_in(streams_of[7], 71), 0),
    }


beta_one = 0.9
beta_two = 0.999
learn_rate = 0.2
decay_rate = 0.5
epsilon = 1e-08

def partial_term(tokens, cot_query, cot_value, weights):
    inv_width = 1.0 / math.sqrt(D)
    inv_rank = 1.0 / math.sqrt(R)
    pieces = []
    for index, cot in ((0, cot_query), (1, cot_value)):
        down = weights[2 * index * R:(2 * index + 1) * R]
        up_rows = weights[(2 * index + 1) * R:(2 * index + 2) * R]
        lowrank = (jnp.dot(tokens, down.T, preferred_element_type=jnp.float32) * inv_width).astype(jnp.bfloat16)
        back = (jnp.dot(cot, up_rows.T, preferred_element_type=jnp.float32) * inv_rank).astype(jnp.bfloat16)
        pieces.append(jnp.dot(back.T, tokens, preferred_element_type=jnp.float32) * inv_width)
        pieces.append(jnp.dot(lowrank.T, cot, preferred_element_type=jnp.float32) * inv_rank)
    return jnp.concatenate(pieces, axis=0)

def group_update(packed):
    tokens, cot_query, cot_value, weights, first, second = packed
    blocks = (tokens.reshape(N_FSDP, TOK_DEV, D), cot_query.reshape(N_FSDP, TOK_DEV, D), cot_value.reshape(N_FSDP, TOK_DEV, D))

    def accumulate(total, block):
        rounded = lax.optimization_barrier(partial_term(block[0], block[1], block[2], weights).astype(jnp.bfloat16))
        return (total + rounded.astype(jnp.float32), None)
    total, _ = lax.scan(accumulate, jnp.zeros((ROWS, D), jnp.float32), blocks)
    gradient = total / TOKG
    params = weights.astype(jnp.float32)
    new_first = beta_one * first.astype(jnp.float32) + (1.0 - beta_one) * gradient
    new_second = beta_two * second.astype(jnp.float32) + (1.0 - beta_two) * gradient * gradient
    first_hat = new_first / (1.0 - beta_one ** 2)
    second_hat = new_second / (1.0 - beta_two ** 2)
    step = first_hat / (jnp.sqrt(second_hat) + epsilon) + decay_rate * params
    return (params - learn_rate * step).astype(jnp.bfloat16)

def reference(hidden, grad_query, grad_value, adapters, first_moment, second_moment, mixing):
    updated = lax.map(group_update, (hidden, grad_query, grad_value, adapters, first_moment, second_moment))
    lower = jnp.roll(updated, 1, axis=0).astype(jnp.float32)
    upper = jnp.roll(updated, -1, axis=0).astype(jnp.float32)
    weights = mixing.astype(jnp.float32)
    total = weights[:, 0, None, None] * lower + weights[:, 1, None, None] * updated.astype(jnp.float32)
    total = total + weights[:, 2, None, None] * upper
    return (total / 4.0).astype(jnp.bfloat16)
```

```python
import functools
import math

import jax
import jax.numpy as jnp
from jax import lax
from jax.experimental import pallas as pl
from jax.experimental.pallas import tpu as pltpu
from jax.sharding import PartitionSpec as P

beta_one = 0.9
beta_two = 0.999
learn_rate = 0.2
decay_rate = 0.5
epsilon = 1e-08

MESH = pl.DeviceIdType.MESH
CHUNKS = 10
LAG_SUM = 2
LAG_MIX = 3


def shifted(array, axis, by):
    length = lax.axis_size(axis)
    return lax.ppermute(array, axis, [(i, (i + by) % length) for i in range(length)])


def contract_tokens(left, right, scale):
    return (
        lax.dot_general(left, right, (((0,), (0,)), ((), ())), preferred_element_type=jnp.float32)
        * scale
    )


def adamw(params, first, second, gradient):
    new_first = beta_one * first + (1.0 - beta_one) * gradient
    new_second = beta_two * second + (1.0 - beta_two) * gradient * gradient
    first_hat = new_first / (1.0 - beta_one**2)
    second_hat = new_second / (1.0 - beta_two**2)
    step = first_hat / (jnp.sqrt(second_hat) + epsilon) + decay_rate * params
    return (params - learn_rate * step).astype(jnp.bfloat16)


def shards(hidden, grad_query, grad_value, adapters, first_moment, second_moment, mixing):
    tokens = hidden[0]
    width = tokens.shape[1]
    full_rows = lax.all_gather(adapters, "fsdp", axis=1, tiled=True)[0]
    rank = full_rows.shape[0] // 4
    inv_width = 1.0 / math.sqrt(width)
    inv_rank = 1.0 / math.sqrt(rank)
    factors = []
    for index, cot in ((0, grad_query[0]), (1, grad_value[0])):
        down = full_rows[2 * index * rank : (2 * index + 1) * rank]
        up_rows = full_rows[(2 * index + 1) * rank : (2 * index + 2) * rank]
        lowrank = (jnp.dot(tokens, down.T, preferred_element_type=jnp.float32) * inv_width).astype(
            jnp.bfloat16
        )
        back = (jnp.dot(cot, up_rows.T, preferred_element_type=jnp.float32) * inv_rank).astype(
            jnp.bfloat16
        )
        factors.append((back, tokens, inv_width))
        factors.append((lowrank, cot, inv_rank))
    group_tokens = tokens.shape[0] * lax.axis_size("fsdp")
    weights = mixing[0].astype(jnp.float32)
    term = jnp.concatenate(
        [contract_tokens(left, right, scale) for left, right, scale in factors], axis=0
    )
    gradient = (
        lax.psum_scatter(
            term.astype(jnp.bfloat16), "fsdp", scatter_dimension=0, tiled=True
        ).astype(jnp.float32)
        / group_tokens
    )
    updated = adamw(
        adapters[0].astype(jnp.float32),
        first_moment[0].astype(jnp.float32),
        second_moment[0].astype(jnp.float32),
        gradient,
    )
    lower = shifted(updated, "blk", 1)
    upper = shifted(updated, "blk", -1)
    total = weights[0] * lower.astype(jnp.float32) + weights[1] * updated.astype(jnp.float32)
    total = total + weights[2] * upper.astype(jnp.float32)
    results = (total / 4.0).astype(jnp.bfloat16)
    return results[None]


def kernel(
    groups,
    x_hbm,
    gq_hbm,
    gv_hbm,
    ad_hbm,
    fm_hbm,
    sm_hbm,
    mix_ref,
    out_ref,
    mats,
    full,
    own,
    first,
    second,
    fac,
    stage,
    sums,
    upd,
    low,
    high,
    ld_sem,
    ag_send,
    ag_recv,
    rs_send,
    rs_recv,
    go_send,
    go_recv,
):
    z = lax.axis_index("fsdp")
    b = lax.axis_index("blk")
    rows, width = ad_hbm.shape
    tokens = x_hbm.shape[0]
    cols = width // CHUNKS
    inv_width = 1.0 / math.sqrt(width)
    inv_rank = 1.0 / math.sqrt(rows)
    group_tokens = tokens * 4
    half = z // 2
    inner = z + 1 - 2 * half
    outer = z - 1 + 2 * half
    is_end = (z == 0) | (z == 3)
    is_mid = (z == 1) | (z == 2)
    above = lax.rem(b + 1, groups)
    below = lax.rem(b + groups - 1, groups)

    def g(s):
        return s + half * (3 - 2 * s)

    def mat_of(s):
        return (s % 2) * (s // 2 + 1)

    def scale_of(s):
        return jnp.where(s % 2 == 0, jnp.float32(inv_width), jnp.float32(inv_rank))

    def span(c):
        return pl.ds(pl.multiple_of(c * cols, 128), cols)

    loads = [
        pltpu.make_async_copy(ad_hbm, own, ld_sem.at[0]),
        pltpu.make_async_copy(x_hbm, mats.at[0], ld_sem.at[1]),
        pltpu.make_async_copy(gq_hbm, mats.at[1], ld_sem.at[2]),
        pltpu.make_async_copy(gv_hbm, mats.at[2], ld_sem.at[3]),
        pltpu.make_async_copy(fm_hbm, first, ld_sem.at[4]),
        pltpu.make_async_copy(sm_hbm, second, ld_sem.at[5]),
    ]
    for load in loads:
        load.start()

    barrier = pltpu.get_barrier_semaphore()
    pl.semaphore_signal(barrier, inc=1, device_id={"fsdp": inner}, device_id_type=MESH)
    pl.semaphore_signal(barrier, inc=1, device_id={"blk": above}, device_id_type=MESH)
    pl.semaphore_signal(barrier, inc=1, device_id={"blk": below}, device_id_type=MESH)

    @pl.when(is_mid)
    def _():
        pl.semaphore_signal(barrier, inc=1, device_id={"fsdp": outer}, device_id_type=MESH)
        pl.semaphore_wait(barrier, 4)

    @pl.when(is_end)
    def _():
        pl.semaphore_wait(barrier, 3)

    def gather(s, src, c, slot, to):
        return pltpu.make_async_remote_copy(
            src_ref=src.at[:, span(c)],
            dst_ref=full.at[s, :, span(c)],
            send_sem=ag_send.at[slot, c],
            recv_sem=ag_recv.at[s, c],
            device_id={"fsdp": to},
            device_id_type=MESH,
        )

    def pass_sum(src_slot, dst_slot, c, to):
        return pltpu.make_async_remote_copy(
            src_ref=stage.at[src_slot, :, span(c)],
            dst_ref=sums.at[dst_slot, :, span(c)],
            send_sem=rs_send.at[src_slot, c],
            recv_sem=rs_recv.at[dst_slot, c],
            device_id={"fsdp": to},
            device_id_type=MESH,
        )

    def gossip(c, way):
        return pltpu.make_async_remote_copy(
            src_ref=upd.at[:, span(c)],
            dst_ref=(low if way == 0 else high).at[:, span(c)],
            send_sem=go_send.at[way, c],
            recv_sem=go_recv.at[way, c],
            device_id={"blk": above if way == 0 else below},
            device_id_type=MESH,
        )

    def wait_shard(s, c):
        gather(s, full.at[s], c, 0, inner).wait_recv()

    def wait_sum(slot, c):
        pass_sum(0, slot, c, inner).wait_recv()

    def each(body):
        def step(c, carry):
            body(c)
            return carry

        lax.fori_loop(0, CHUNKS, step, 0)

    def product(s, block, c):
        return lax.dot_general(
            block,
            mats[mat_of(s), :, span(c)],
            (((1,), (1,)), ((), ())),
            preferred_element_type=jnp.float32,
        )

    def keep(s, acc):
        fac[s + 1 - 2 * (s % 2)] = (acc * scale_of(s)).astype(jnp.bfloat16)

    zero = jnp.zeros((rows, tokens), jnp.float32)

    def own_factor(s):
        keep(s, lax.fori_loop(0, CHUNKS, lambda c, acc: acc + product(s, own[:, span(c)], c), zero))

    def partial(k, c):
        return (
            jnp.dot(fac[k], mats[mat_of(k), :, span(c)], preferred_element_type=jnp.float32)
            * scale_of(k)
        )

    def finish(c, total):
        at = span(c)
        upd[:, at] = adamw(
            own[:, at].astype(jnp.float32),
            first[:, at].astype(jnp.float32),
            second[:, at].astype(jnp.float32),
            total / group_tokens,
        )
        gossip(c, 0).start()
        gossip(c, 1).start()

    weights = [mix_ref[0, j].astype(jnp.float32) for j in range(3)]

    def mix(c):
        at = span(c)
        gossip(c, 0).wait_recv()
        gossip(c, 1).wait_recv()
        total = weights[0] * low[:, at].astype(jnp.float32) + weights[1] * upd[:, at].astype(
            jnp.float32
        )
        total = total + weights[2] * high[:, at].astype(jnp.float32)
        out_ref[:, at] = (total / 4.0).astype(jnp.bfloat16)

    @pl.when(is_end)
    def _end():
        each(lambda c: gather(g(0), ad_hbm, c, 0, inner).start())
        for load in loads:
            load.wait()
        own_factor(g(0))

        def send_partial(slot, k):
            def body(c):
                stage[slot, :, span(c)] = partial(k, c).astype(jnp.bfloat16)
                pass_sum(slot, slot, c, inner).start()

            each(body)

        def receive(s):
            def body(c, acc):
                wait_shard(s, c)
                return acc + product(s, full[s, :, span(c)], c)

            keep(s, lax.fori_loop(0, CHUNKS, body, zero))

        send_partial(0, g(1))
        receive(g(1))
        receive(g(2))
        send_partial(1, g(3))
        receive(g(3))
        send_partial(2, g(2))

        def last(t, carry):
            @pl.when(t < CHUNKS)
            def _():
                wait_sum(0, t)
                finish(t, sums[0, :, span(t)].astype(jnp.float32) + partial(g(0), t))

            @pl.when(t >= LAG_MIX)
            def _():
                mix(t - LAG_MIX)

            return carry

        lax.fori_loop(0, CHUNKS + LAG_MIX, last, 0)
        each(lambda c: gather(g(0), ad_hbm, c, 0, inner).wait_send())

    @pl.when(is_mid)
    def _mid():
        def send_own(c):
            gather(g(1), ad_hbm, c, 0, outer).start()
            gather(g(1), ad_hbm, c, 1, inner).start()

        each(send_own)
        for load in loads:
            load.wait()
        own_factor(g(1))

        def near(c, accs):
            wait_shard(g(0), c)
            gather(g(0), full.at[g(0)], c, 2, inner).start()
            wait_shard(g(2), c)
            gather(g(2), full.at[g(2)], c, 3, outer).start()
            return (
                accs[0] + product(g(0), full[g(0), :, span(c)], c),
                accs[1] + product(g(2), full[g(2), :, span(c)], c),
            )

        acc_zero, acc_two = lax.fori_loop(0, CHUNKS, near, (zero, zero))
        keep(g(0), acc_zero)
        keep(g(2), acc_two)

        def far(c, acc):
            wait_shard(g(3), c)
            gather(g(3), full.at[g(3)], c, 4, outer).start()
            return acc + product(g(3), full[g(3), :, span(c)], c)

        keep(g(3), lax.fori_loop(0, CHUNKS, far, zero))

        def last(t, carry):
            @pl.when(t < 2 * CHUNKS)
            def _():
                m, c = t // CHUNKS, t % CHUNKS
                wait_sum(1 + m, c)
                total = sums[1 + m, :, span(c)].astype(jnp.float32) + partial(g(3 - m), c)
                stage[m, :, span(c)] = total.astype(jnp.bfloat16)
                pass_sum(m, 3 + m, c, inner).start()

            @pl.when((t >= LAG_SUM) & (t < CHUNKS + LAG_SUM))
            def _():
                c = t - LAG_SUM
                wait_sum(3, c)
                total = sums[3, :, span(c)].astype(jnp.float32) + partial(g(0), c)
                stage[2, :, span(c)] = total.astype(jnp.bfloat16)
                pass_sum(2, 0, c, outer).start()

            @pl.when((t >= CHUNKS + LAG_SUM) & (t < 2 * CHUNKS + LAG_SUM))
            def _():
                c = t - CHUNKS - LAG_SUM
                wait_sum(0, c)
                wait_sum(4, c)
                total = sums[0, :, span(c)].astype(jnp.float32) + partial(g(1), c)
                finish(c, total + sums[4, :, span(c)].astype(jnp.float32))

            @pl.when(t >= CHUNKS + LAG_SUM + LAG_MIX)
            def _():
                mix(t - CHUNKS - LAG_SUM - LAG_MIX)

            return carry

        lax.fori_loop(0, 2 * CHUNKS + LAG_SUM + LAG_MIX, last, 0)

        def sent(c):
            for slot in range(5):
                gather(g(1), ad_hbm, c, slot, inner).wait_send()

        each(sent)

    def drained(c):
        for slot in range(3):
            pass_sum(slot, 0, c, inner).wait_send()
        gossip(c, 0).wait_send()
        gossip(c, 1).wait_send()

    each(drained)


def fused(hidden, grad_query, grad_value, adapters, first_moment, second_moment, mixing):
    _, tokens, width = hidden.shape
    rows = adapters.shape[1]
    groups = lax.axis_size("blk")
    bf16 = jnp.bfloat16
    anywhere = pl.BlockSpec(memory_space=pl.ANY)
    shard = pltpu.VMEM((rows, width), bf16)
    out = pl.pallas_call(
        functools.partial(kernel, groups),
        out_shape=jax.ShapeDtypeStruct((rows, width), bf16),
        in_specs=[anywhere] * 6 + [pl.BlockSpec(memory_space=pltpu.SMEM)],
        out_specs=pl.BlockSpec(memory_space=pltpu.VMEM),
        scratch_shapes=[
            pltpu.VMEM((3, tokens, width), bf16),
            pltpu.VMEM((4, rows, width), bf16),
            shard,
            shard,
            shard,
            pltpu.VMEM((4, rows, tokens), bf16),
            pltpu.VMEM((3, rows, width), bf16),
            pltpu.VMEM((5, rows, width), bf16),
            shard,
            shard,
            shard,
            pltpu.SemaphoreType.DMA((6,)),
            pltpu.SemaphoreType.DMA((5, CHUNKS)),
            pltpu.SemaphoreType.DMA((4, CHUNKS)),
            pltpu.SemaphoreType.DMA((3, CHUNKS)),
            pltpu.SemaphoreType.DMA((5, CHUNKS)),
            pltpu.SemaphoreType.DMA((2, CHUNKS)),
            pltpu.SemaphoreType.DMA((2, CHUNKS)),
        ],
        compiler_params=pltpu.CompilerParams(collective_id=0, has_side_effects=True),
    )(
        hidden[0],
        grad_query[0],
        grad_value[0],
        adapters[0],
        first_moment[0],
        second_moment[0],
        mixing,
    )
    return out[None]


def solution(mesh):
    spec = P("blk", "fsdp", None)
    in_specs = (spec,) * 6 + (P("blk", None),)
    body = fused if mesh.shape["fsdp"] == 4 and mesh.shape["blk"] > 2 else shards
    return jax.shard_map(body, mesh=mesh, in_specs=in_specs, out_specs=spec, check_vma=False)
```

```python
import functools
import math

import jax
import jax.numpy as jnp
from jax import lax
from jax.experimental import pallas as pl
from jax.experimental.pallas import tpu as pltpu
from jax.sharding import PartitionSpec as P

beta_one = 0.9
beta_two = 0.999
learn_rate = 0.2
decay_rate = 0.5
epsilon = 1e-08

MESH = pl.DeviceIdType.MESH
PARTS = 3
STRIPS = 4
CHUNKS = PARTS * STRIPS
HEAD = 2 * STRIPS
AHEAD = 3
LAG_SUM = 4
LAG_MIX = 5


def shifted(array, axis, by):
    length = lax.axis_size(axis)
    return lax.ppermute(array, axis, [(i, (i + by) % length) for i in range(length)])


def contract_tokens(left, right, scale):
    return (
        lax.dot_general(left, right, (((0,), (0,)), ((), ())), preferred_element_type=jnp.float32)
        * scale
    )


def adamw(params, first, second, gradient):
    new_first = beta_one * first + (1.0 - beta_one) * gradient
    new_second = beta_two * second + (1.0 - beta_two) * gradient * gradient
    first_hat = new_first / (1.0 - beta_one**2)
    second_hat = new_second / (1.0 - beta_two**2)
    step = first_hat / (jnp.sqrt(second_hat) + epsilon) + decay_rate * params
    return (params - learn_rate * step).astype(jnp.bfloat16)


def shards(hidden, grad_query, grad_value, adapters, first_moment, second_moment, mixing):
    tokens = hidden[0]
    width = tokens.shape[1]
    full_rows = lax.all_gather(adapters, "fsdp", axis=1, tiled=True)[0]
    rank = full_rows.shape[0] // 4
    inv_width = 1.0 / math.sqrt(width)
    inv_rank = 1.0 / math.sqrt(rank)
    factors = []
    for index, cot in ((0, grad_query[0]), (1, grad_value[0])):
        down = full_rows[2 * index * rank : (2 * index + 1) * rank]
        up_rows = full_rows[(2 * index + 1) * rank : (2 * index + 2) * rank]
        lowrank = (jnp.dot(tokens, down.T, preferred_element_type=jnp.float32) * inv_width).astype(
            jnp.bfloat16
        )
        back = (jnp.dot(cot, up_rows.T, preferred_element_type=jnp.float32) * inv_rank).astype(
            jnp.bfloat16
        )
        factors.append((back, tokens, inv_width))
        factors.append((lowrank, cot, inv_rank))
    group_tokens = tokens.shape[0] * lax.axis_size("fsdp")
    weights = mixing[0].astype(jnp.float32)
    term = jnp.concatenate(
        [contract_tokens(left, right, scale) for left, right, scale in factors], axis=0
    )
    gradient = (
        lax.psum_scatter(
            term.astype(jnp.bfloat16), "fsdp", scatter_dimension=0, tiled=True
        ).astype(jnp.float32)
        / group_tokens
    )
    updated = adamw(
        adapters[0].astype(jnp.float32),
        first_moment[0].astype(jnp.float32),
        second_moment[0].astype(jnp.float32),
        gradient,
    )
    lower = shifted(updated, "blk", 1)
    upper = shifted(updated, "blk", -1)
    total = weights[0] * lower.astype(jnp.float32) + weights[1] * updated.astype(jnp.float32)
    total = total + weights[2] * upper.astype(jnp.float32)
    results = (total / 4.0).astype(jnp.bfloat16)
    return results[None]


def kernel(
    groups,
    x_hbm,
    gq_hbm,
    gv_hbm,
    ad_hbm,
    fm_hbm,
    sm_hbm,
    mix_ref,
    out_ref,
    mats,
    full,
    own,
    first,
    second,
    fac,
    acc,
    stage,
    sums,
    upd,
    low,
    high,
    ld_sem,
    ag_send,
    ag_recv,
    rs_send,
    rs_recv,
    go_send,
    go_recv,
):
    z = lax.axis_index("fsdp")
    b = lax.axis_index("blk")
    rows, width = ad_hbm.shape
    tokens = x_hbm.shape[0]
    cols = width // STRIPS
    part_rows = rows // PARTS
    inv_width = 1.0 / math.sqrt(width)
    inv_rank = 1.0 / math.sqrt(rows)
    group_tokens = tokens * 4
    half = z // 2
    inner = z + 1 - 2 * half
    outer = z - 1 + 2 * half
    is_end = (z == 0) | (z == 3)
    is_mid = (z == 1) | (z == 2)
    above = lax.rem(b + 1, groups)
    below = lax.rem(b + groups - 1, groups)

    def g(s):
        return s + half * (3 - 2 * s)

    def mat_of(s):
        return (s % 2) * (s // 2 + 1)

    def scale_of(s):
        return jnp.where(s % 2 == 0, jnp.float32(inv_width), jnp.float32(inv_rank))

    def span(c):
        return pl.ds(pl.multiple_of((c % STRIPS) * cols, 128), cols)

    def block(c):
        return pl.ds(pl.multiple_of((c // STRIPS) * part_rows, part_rows), part_rows), span(c)

    loads = [
        pltpu.make_async_copy(ad_hbm, own, ld_sem.at[0]),
        pltpu.make_async_copy(x_hbm, mats.at[0], ld_sem.at[1]),
        pltpu.make_async_copy(gq_hbm, mats.at[1], ld_sem.at[2]),
        pltpu.make_async_copy(gv_hbm, mats.at[2], ld_sem.at[3]),
        pltpu.make_async_copy(fm_hbm, first, ld_sem.at[4]),
        pltpu.make_async_copy(sm_hbm, second, ld_sem.at[5]),
    ]
    for load in loads:
        load.start()

    barrier = pltpu.get_barrier_semaphore()
    pl.semaphore_signal(barrier, inc=1, device_id={"fsdp": inner}, device_id_type=MESH)
    pl.semaphore_signal(barrier, inc=1, device_id={"blk": above}, device_id_type=MESH)
    pl.semaphore_signal(barrier, inc=1, device_id={"blk": below}, device_id_type=MESH)

    @pl.when(is_mid)
    def _():
        pl.semaphore_signal(barrier, inc=1, device_id={"fsdp": outer}, device_id_type=MESH)
        pl.semaphore_wait(barrier, 4)

    @pl.when(is_end)
    def _():
        pl.semaphore_wait(barrier, 3)

    def gather(s, src, c, slot, to):
        return pltpu.make_async_remote_copy(
            src_ref=src,
            dst_ref=full.at[s, c],
            send_sem=ag_send.at[slot, c],
            recv_sem=ag_recv.at[s, c],
            device_id={"fsdp": to},
            device_id_type=MESH,
        )

    def pass_sum(src_slot, dst_slot, c, to):
        return pltpu.make_async_remote_copy(
            src_ref=stage.at[src_slot, c],
            dst_ref=sums.at[dst_slot, c],
            send_sem=rs_send.at[src_slot, c],
            recv_sem=rs_recv.at[dst_slot, c],
            device_id={"fsdp": to},
            device_id_type=MESH,
        )

    def gossip(c, way):
        return pltpu.make_async_remote_copy(
            src_ref=upd.at[c],
            dst_ref=(low if way == 0 else high).at[c],
            send_sem=go_send.at[way, c],
            recv_sem=go_recv.at[way, c],
            device_id={"blk": above if way == 0 else below},
            device_id_type=MESH,
        )

    def wait_shard(s, c):
        gather(s, full.at[s, c], c, 0, inner).wait_recv()

    def wait_sum(slot, c):
        pass_sum(0, slot, c, inner).wait_recv()

    def each(body, begin=0, end=CHUNKS):
        def step(c, carry):
            body(c)
            return carry

        lax.fori_loop(begin, end, step, 0)

    def product(s, left, c):
        return lax.dot_general(
            left,
            mats[mat_of(s), :, span(c)],
            (((1,), (1,)), ((), ())),
            preferred_element_type=jnp.float32,
        )

    def partner(s):
        return s + 1 - 2 * (s % 2)

    def absorb(s, slot, c):
        term = product(s, full[s, c], c)

        @pl.when(c % STRIPS == 0)
        def _():
            acc[slot] = term

        @pl.when(c % STRIPS > 0)
        def _():
            acc[slot] += term

        @pl.when(c % STRIPS == STRIPS - 1)
        def _():
            fac[partner(s), c // STRIPS] = (acc[slot] * scale_of(s)).astype(jnp.bfloat16)

    def own_factor(s):
        zero = jnp.zeros((rows, tokens), jnp.float32)
        whole = lax.fori_loop(
            0, STRIPS, lambda c, total: total + product(s, own[:, span(c)], c), zero
        )
        whole = (whole * scale_of(s)).astype(jnp.bfloat16)
        for p in range(PARTS):
            fac[partner(s), p] = whole[p * part_rows : (p + 1) * part_rows]

    def partial(k, c):
        return (
            jnp.dot(
                fac[k, c // STRIPS],
                mats[mat_of(k), :, span(c)],
                preferred_element_type=jnp.float32,
            )
            * scale_of(k)
        )

    def finish(c, total):
        at = block(c)
        upd[c] = adamw(
            own[at].astype(jnp.float32),
            first[at].astype(jnp.float32),
            second[at].astype(jnp.float32),
            total / group_tokens,
        )
        gossip(c, 0).start()
        gossip(c, 1).start()

    weights = [mix_ref[0, j].astype(jnp.float32) for j in range(3)]

    def mix(c):
        at = block(c)
        gossip(c, 0).wait_recv()
        gossip(c, 1).wait_recv()
        total = weights[0] * low[c].astype(jnp.float32) + weights[1] * upd[c].astype(
            jnp.float32
        )
        total = total + weights[2] * high[c].astype(jnp.float32)
        out_ref[at] = (total / 4.0).astype(jnp.bfloat16)

    @pl.when(is_end)
    def _end():
        each(lambda c: gather(g(0), ad_hbm.at[block(c)], c, 0, inner).start())
        for load in loads:
            load.wait()
        own_factor(g(0))

        def send_partial(slot, k, c):
            stage[slot, c] = partial(k, c).astype(jnp.bfloat16)
            pass_sum(slot, slot, c, inner).start()

        def receive(s, slot=None, k=None):
            def body(c):
                wait_shard(s, c)
                absorb(s, 0, c)
                if slot is not None:

                    @pl.when(c % STRIPS == STRIPS - 1)
                    def _():
                        for j in range(STRIPS):
                            send_partial(slot, k, c - (STRIPS - 1) + j)

            each(body)

        each(lambda c: send_partial(0, g(1), c), 0, HEAD)
        receive(g(1))
        receive(g(2), 1, g(3))
        receive(g(3), 2, g(2))
        each(lambda c: send_partial(0, g(1), c), HEAD, CHUNKS)

        def last(t, carry):
            @pl.when(t < CHUNKS)
            def _():
                wait_sum(0, t)
                finish(t, sums[0, t].astype(jnp.float32) + partial(g(0), t))

            @pl.when(t >= LAG_MIX)
            def _():
                mix(t - LAG_MIX)

            return carry

        lax.fori_loop(0, CHUNKS + LAG_MIX, last, 0)
        each(lambda c: gather(g(0), ad_hbm.at[block(c)], c, 0, inner).wait_send())

    @pl.when(is_mid)
    def _mid():
        def send_own(c):
            gather(g(1), ad_hbm.at[block(c)], c, 0, outer).start()
            gather(g(1), ad_hbm.at[block(c)], c, 1, inner).start()

        each(send_own)
        for load in loads:
            load.wait()
        own_factor(g(1))

        def near(c):
            wait_shard(g(0), c)
            gather(g(0), full.at[g(0), c], c, 2, inner).start()
            wait_shard(g(2), c)
            gather(g(2), full.at[g(2), c], c, 3, outer).start()
            absorb(g(0), 0, c)
            absorb(g(2), 1, c)

        each(near)

        def far(c):
            wait_shard(g(3), c)
            gather(g(3), full.at[g(3), c], c, 4, outer).start()
            absorb(g(3), 0, c)

        each(far, 0, CHUNKS - AHEAD)

        def last(t, carry):
            @pl.when(t < AHEAD)
            def _():
                far(t + CHUNKS - AHEAD)

            @pl.when(t < 2 * CHUNKS)
            def _():
                m, c = t // CHUNKS, t % CHUNKS
                wait_sum(1 + m, c)
                total = sums[1 + m, c].astype(jnp.float32) + partial(g(3 - m), c)
                stage[m, c] = total.astype(jnp.bfloat16)
                pass_sum(m, 3 + m, c, inner).start()

            @pl.when((t >= LAG_SUM) & (t < CHUNKS + LAG_SUM))
            def _():
                c = t - LAG_SUM
                wait_sum(3, c)
                total = sums[3, c].astype(jnp.float32) + partial(g(0), c)
                stage[2, c] = total.astype(jnp.bfloat16)
                pass_sum(2, 0, c, outer).start()

            @pl.when((t >= CHUNKS + LAG_SUM) & (t < 2 * CHUNKS + LAG_SUM))
            def _():
                c = t - CHUNKS - LAG_SUM
                wait_sum(0, c)
                wait_sum(4, c)
                total = sums[0, c].astype(jnp.float32) + partial(g(1), c)
                finish(c, total + sums[4, c].astype(jnp.float32))

            @pl.when(t >= CHUNKS + LAG_SUM + LAG_MIX)
            def _():
                mix(t - CHUNKS - LAG_SUM - LAG_MIX)

            return carry

        lax.fori_loop(0, 2 * CHUNKS + LAG_SUM + LAG_MIX, last, 0)

        def sent(c):
            for slot in range(5):
                gather(g(1), ad_hbm.at[block(c)], c, slot, inner).wait_send()

        each(sent)

    def drained(c):
        for slot in range(3):
            pass_sum(slot, 0, c, inner).wait_send()
        gossip(c, 0).wait_send()
        gossip(c, 1).wait_send()

    each(drained)


def fused(hidden, grad_query, grad_value, adapters, first_moment, second_moment, mixing):
    _, tokens, width = hidden.shape
    rows = adapters.shape[1]
    groups = lax.axis_size("blk")
    bf16 = jnp.bfloat16
    anywhere = pl.BlockSpec(memory_space=pl.ANY)
    shard = pltpu.VMEM((rows, width), bf16)
    chunks = (CHUNKS, rows // PARTS, width // STRIPS)
    out = pl.pallas_call(
        functools.partial(kernel, groups),
        out_shape=jax.ShapeDtypeStruct((rows, width), bf16),
        in_specs=[anywhere] * 6 + [pl.BlockSpec(memory_space=pltpu.SMEM)],
        out_specs=pl.BlockSpec(memory_space=pltpu.VMEM),
        scratch_shapes=[
            pltpu.VMEM((3, tokens, width), bf16),
            pltpu.VMEM((4, *chunks), bf16),
            shard,
            shard,
            shard,
            pltpu.VMEM((4, PARTS, rows // PARTS, tokens), bf16),
            pltpu.VMEM((2, rows // PARTS, tokens), jnp.float32),
            pltpu.VMEM((3, *chunks), bf16),
            pltpu.VMEM((5, *chunks), bf16),
            pltpu.VMEM(chunks, bf16),
            pltpu.VMEM(chunks, bf16),
            pltpu.VMEM(chunks, bf16),
            pltpu.SemaphoreType.DMA((6,)),
            pltpu.SemaphoreType.DMA((5, CHUNKS)),
            pltpu.SemaphoreType.DMA((4, CHUNKS)),
            pltpu.SemaphoreType.DMA((3, CHUNKS)),
            pltpu.SemaphoreType.DMA((5, CHUNKS)),
            pltpu.SemaphoreType.DMA((2, CHUNKS)),
            pltpu.SemaphoreType.DMA((2, CHUNKS)),
        ],
        compiler_params=pltpu.CompilerParams(collective_id=0, has_side_effects=True),
    )(
        hidden[0],
        grad_query[0],
        grad_value[0],
        adapters[0],
        first_moment[0],
        second_moment[0],
        mixing,
    )
    return out[None]


def solution(mesh):
    spec = P("blk", "fsdp", None)
    in_specs = (spec,) * 6 + (P("blk", None),)
    body = fused if mesh.shape["fsdp"] == 4 and mesh.shape["blk"] > 2 else shards
    return jax.shard_map(body, mesh=mesh, in_specs=in_specs, out_specs=spec, check_vma=False)
```

```python
import functools
import math

import jax
import jax.numpy as jnp
from jax import lax
from jax.experimental import pallas as pl
from jax.experimental.pallas import tpu as pltpu
from jax.sharding import PartitionSpec as P

beta_one = 0.9
beta_two = 0.999
learn_rate = 0.2
decay_rate = 0.5
epsilon = 1e-08

MESH = pl.DeviceIdType.MESH
PARTS = 3
STRIPS = 2
CHUNKS = PARTS * STRIPS
HEAD = 2 * STRIPS
AHEAD = 2
LAG_SUM = 2
LAG_MIX = 3


def shifted(array, axis, by):
    length = lax.axis_size(axis)
    return lax.ppermute(array, axis, [(i, (i + by) % length) for i in range(length)])


def contract_tokens(left, right, scale):
    return (
        lax.dot_general(left, right, (((0,), (0,)), ((), ())), preferred_element_type=jnp.float32)
        * scale
    )


def adamw(params, first, second, gradient):
    new_first = beta_one * first + (1.0 - beta_one) * gradient
    new_second = beta_two * second + (1.0 - beta_two) * gradient * gradient
    first_hat = new_first / (1.0 - beta_one**2)
    second_hat = new_second / (1.0 - beta_two**2)
    step = first_hat / (jnp.sqrt(second_hat) + epsilon) + decay_rate * params
    return (params - learn_rate * step).astype(jnp.bfloat16)


def shards(hidden, grad_query, grad_value, adapters, first_moment, second_moment, mixing):
    tokens = hidden[0]
    width = tokens.shape[1]
    full_rows = lax.all_gather(adapters, "fsdp", axis=1, tiled=True)[0]
    rank = full_rows.shape[0] // 4
    inv_width = 1.0 / math.sqrt(width)
    inv_rank = 1.0 / math.sqrt(rank)
    factors = []
    for index, cot in ((0, grad_query[0]), (1, grad_value[0])):
        down = full_rows[2 * index * rank : (2 * index + 1) * rank]
        up_rows = full_rows[(2 * index + 1) * rank : (2 * index + 2) * rank]
        lowrank = (jnp.dot(tokens, down.T, preferred_element_type=jnp.float32) * inv_width).astype(
            jnp.bfloat16
        )
        back = (jnp.dot(cot, up_rows.T, preferred_element_type=jnp.float32) * inv_rank).astype(
            jnp.bfloat16
        )
        factors.append((back, tokens, inv_width))
        factors.append((lowrank, cot, inv_rank))
    group_tokens = tokens.shape[0] * lax.axis_size("fsdp")
    weights = mixing[0].astype(jnp.float32)
    term = jnp.concatenate(
        [contract_tokens(left, right, scale) for left, right, scale in factors], axis=0
    )
    gradient = (
        lax.psum_scatter(
            term.astype(jnp.bfloat16), "fsdp", scatter_dimension=0, tiled=True
        ).astype(jnp.float32)
        / group_tokens
    )
    updated = adamw(
        adapters[0].astype(jnp.float32),
        first_moment[0].astype(jnp.float32),
        second_moment[0].astype(jnp.float32),
        gradient,
    )
    lower = shifted(updated, "blk", 1)
    upper = shifted(updated, "blk", -1)
    total = weights[0] * lower.astype(jnp.float32) + weights[1] * updated.astype(jnp.float32)
    total = total + weights[2] * upper.astype(jnp.float32)
    results = (total / 4.0).astype(jnp.bfloat16)
    return results[None]


def kernel(
    groups,
    x_hbm,
    gq_hbm,
    gv_hbm,
    ad_hbm,
    fm_hbm,
    sm_hbm,
    mix_ref,
    out_ref,
    mats,
    full,
    own,
    first,
    second,
    fac,
    acc,
    stage,
    sums,
    upd,
    low,
    high,
    ld_sem,
    ag_send,
    ag_recv,
    rs_send,
    rs_recv,
    go_send,
    go_recv,
):
    z = lax.axis_index("fsdp")
    b = lax.axis_index("blk")
    rows, width = ad_hbm.shape
    tokens = x_hbm.shape[0]
    cols = width // STRIPS
    part_rows = rows // PARTS
    inv_width = 1.0 / math.sqrt(width)
    inv_rank = 1.0 / math.sqrt(rows)
    group_tokens = tokens * 4
    half = z // 2
    inner = z + 1 - 2 * half
    outer = z - 1 + 2 * half
    is_end = (z == 0) | (z == 3)
    is_mid = (z == 1) | (z == 2)
    above = lax.rem(b + 1, groups)
    below = lax.rem(b + groups - 1, groups)

    def g(s):
        return s + half * (3 - 2 * s)

    def mat_of(s):
        return (s % 2) * (s // 2 + 1)

    def scale_of(s):
        return jnp.where(s % 2 == 0, jnp.float32(inv_width), jnp.float32(inv_rank))

    def span(c):
        return pl.ds(pl.multiple_of((c % STRIPS) * cols, 128), cols)

    def block(c):
        return pl.ds(pl.multiple_of((c // STRIPS) * part_rows, part_rows), part_rows), span(c)

    loads = [
        pltpu.make_async_copy(ad_hbm, own, ld_sem.at[0]),
        pltpu.make_async_copy(x_hbm, mats.at[0], ld_sem.at[1]),
        pltpu.make_async_copy(gq_hbm, mats.at[1], ld_sem.at[2]),
        pltpu.make_async_copy(gv_hbm, mats.at[2], ld_sem.at[3]),
        pltpu.make_async_copy(fm_hbm, first, ld_sem.at[4]),
        pltpu.make_async_copy(sm_hbm, second, ld_sem.at[5]),
    ]
    for load in loads:
        load.start()

    barrier = pltpu.get_barrier_semaphore()
    pl.semaphore_signal(barrier, inc=1, device_id={"fsdp": inner}, device_id_type=MESH)
    pl.semaphore_signal(barrier, inc=1, device_id={"blk": above}, device_id_type=MESH)
    pl.semaphore_signal(barrier, inc=1, device_id={"blk": below}, device_id_type=MESH)

    @pl.when(is_mid)
    def _():
        pl.semaphore_signal(barrier, inc=1, device_id={"fsdp": outer}, device_id_type=MESH)
        pl.semaphore_wait(barrier, 4)

    @pl.when(is_end)
    def _():
        pl.semaphore_wait(barrier, 3)

    def gather(s, src, c, slot, to):
        return pltpu.make_async_remote_copy(
            src_ref=src,
            dst_ref=full.at[s, c],
            send_sem=ag_send.at[slot, c],
            recv_sem=ag_recv.at[s, c],
            device_id={"fsdp": to},
            device_id_type=MESH,
        )

    def pass_sum(src_slot, dst_slot, c, to):
        return pltpu.make_async_remote_copy(
            src_ref=stage.at[src_slot, c],
            dst_ref=sums.at[dst_slot, c],
            send_sem=rs_send.at[src_slot, c],
            recv_sem=rs_recv.at[dst_slot, c],
            device_id={"fsdp": to},
            device_id_type=MESH,
        )

    def gossip(c, way):
        return pltpu.make_async_remote_copy(
            src_ref=upd.at[c],
            dst_ref=(low if way == 0 else high).at[c],
            send_sem=go_send.at[way, c],
            recv_sem=go_recv.at[way, c],
            device_id={"blk": above if way == 0 else below},
            device_id_type=MESH,
        )

    def wait_shard(s, c):
        gather(s, full.at[s, c], c, 0, inner).wait_recv()

    def wait_sum(slot, c):
        pass_sum(0, slot, c, inner).wait_recv()

    def each(body, begin=0, end=CHUNKS):
        def step(c, carry):
            body(c)
            return carry

        lax.fori_loop(begin, end, step, 0)

    def product(s, left, c):
        return lax.dot_general(
            left,
            mats[mat_of(s), :, span(c)],
            (((1,), (1,)), ((), ())),
            preferred_element_type=jnp.float32,
        )

    def partner(s):
        return s + 1 - 2 * (s % 2)

    def absorb(s, slot, c):
        term = product(s, full[s, c], c)

        @pl.when(c % STRIPS == 0)
        def _():
            acc[slot] = term

        @pl.when(c % STRIPS > 0)
        def _():
            acc[slot] += term

        @pl.when(c % STRIPS == STRIPS - 1)
        def _():
            fac[partner(s), c // STRIPS] = (acc[slot] * scale_of(s)).astype(jnp.bfloat16)

    def own_factor(s):
        zero = jnp.zeros((rows, tokens), jnp.float32)
        whole = lax.fori_loop(
            0, STRIPS, lambda c, total: total + product(s, own[:, span(c)], c), zero
        )
        whole = (whole * scale_of(s)).astype(jnp.bfloat16)
        for p in range(PARTS):
            fac[partner(s), p] = whole[p * part_rows : (p + 1) * part_rows]

    def partial(k, c):
        return (
            jnp.dot(
                fac[k, c // STRIPS],
                mats[mat_of(k), :, span(c)],
                preferred_element_type=jnp.float32,
            )
            * scale_of(k)
        )

    def finish(c, total):
        at = block(c)
        upd[c] = adamw(
            own[at].astype(jnp.float32),
            first[at].astype(jnp.float32),
            second[at].astype(jnp.float32),
            total / group_tokens,
        )
        gossip(c, 0).start()
        gossip(c, 1).start()

    weights = [mix_ref[0, j].astype(jnp.float32) for j in range(3)]

    def mix(c):
        at = block(c)
        gossip(c, 0).wait_recv()
        gossip(c, 1).wait_recv()
        total = weights[0] * low[c].astype(jnp.float32) + weights[1] * upd[c].astype(
            jnp.float32
        )
        total = total + weights[2] * high[c].astype(jnp.float32)
        out_ref[at] = (total / 4.0).astype(jnp.bfloat16)

    @pl.when(is_end)
    def _end():
        loads[0].wait()
        each(lambda c: gather(g(0), own.at[block(c)], c, 0, inner).start())
        for load in loads[1:]:
            load.wait()
        own_factor(g(0))

        def send_partial(slot, k, c):
            stage[slot, c] = partial(k, c).astype(jnp.bfloat16)
            pass_sum(slot, slot, c, inner).start()

        def receive(s, slot=None, k=None):
            def body(c):
                wait_shard(s, c)
                absorb(s, 0, c)
                if slot is not None:

                    @pl.when(c % STRIPS == STRIPS - 1)
                    def _():
                        for j in range(STRIPS):
                            send_partial(slot, k, c - (STRIPS - 1) + j)

            each(body)

        each(lambda c: send_partial(0, g(1), c), 0, HEAD)
        receive(g(1))
        receive(g(2), 1, g(3))
        receive(g(3), 2, g(2))
        each(lambda c: send_partial(0, g(1), c), HEAD, CHUNKS)

        def last(t, carry):
            @pl.when(t < CHUNKS)
            def _():
                wait_sum(0, t)
                finish(t, sums[0, t].astype(jnp.float32) + partial(g(0), t))

            @pl.when(t >= LAG_MIX)
            def _():
                mix(t - LAG_MIX)

            return carry

        lax.fori_loop(0, CHUNKS + LAG_MIX, last, 0)
        each(lambda c: gather(g(0), own.at[block(c)], c, 0, inner).wait_send())

    @pl.when(is_mid)
    def _mid():
        def send_own(c):
            gather(g(1), own.at[block(c)], c, 0, outer).start()
            gather(g(1), own.at[block(c)], c, 1, inner).start()

        loads[0].wait()
        each(send_own)
        for load in loads[1:]:
            load.wait()
        own_factor(g(1))

        def near(c):
            wait_shard(g(0), c)
            gather(g(0), full.at[g(0), c], c, 2, inner).start()
            wait_shard(g(2), c)
            gather(g(2), full.at[g(2), c], c, 3, outer).start()
            absorb(g(0), 0, c)
            absorb(g(2), 1, c)

        each(near)

        def far(c):
            wait_shard(g(3), c)
            gather(g(3), full.at[g(3), c], c, 4, outer).start()
            absorb(g(3), 0, c)

        each(far, 0, CHUNKS - AHEAD)

        def last(t, carry):
            @pl.when(t < AHEAD)
            def _():
                far(t + CHUNKS - AHEAD)

            @pl.when(t < 2 * CHUNKS)
            def _():
                m, c = t // CHUNKS, t % CHUNKS
                wait_sum(1 + m, c)
                total = sums[1 + m, c].astype(jnp.float32) + partial(g(3 - m), c)
                stage[m, c] = total.astype(jnp.bfloat16)
                pass_sum(m, 3 + m, c, inner).start()

            @pl.when((t >= LAG_SUM) & (t < CHUNKS + LAG_SUM))
            def _():
                c = t - LAG_SUM
                wait_sum(3, c)
                total = sums[3, c].astype(jnp.float32) + partial(g(0), c)
                stage[2, c] = total.astype(jnp.bfloat16)
                pass_sum(2, 0, c, outer).start()

            @pl.when((t >= CHUNKS + LAG_SUM) & (t < 2 * CHUNKS + LAG_SUM))
            def _():
                c = t - CHUNKS - LAG_SUM
                wait_sum(0, c)
                wait_sum(4, c)
                total = sums[0, c].astype(jnp.float32) + partial(g(1), c)
                finish(c, total + sums[4, c].astype(jnp.float32))

            @pl.when(t >= CHUNKS + LAG_SUM + LAG_MIX)
            def _():
                mix(t - CHUNKS - LAG_SUM - LAG_MIX)

            return carry

        lax.fori_loop(0, 2 * CHUNKS + LAG_SUM + LAG_MIX, last, 0)

        def sent(c):
            for slot in range(5):
                gather(g(1), own.at[block(c)], c, slot, inner).wait_send()

        each(sent)

    def drained(c):
        for slot in range(3):
            pass_sum(slot, 0, c, inner).wait_send()
        gossip(c, 0).wait_send()
        gossip(c, 1).wait_send()

    each(drained)


def fused(hidden, grad_query, grad_value, adapters, first_moment, second_moment, mixing):
    _, tokens, width = hidden.shape
    rows = adapters.shape[1]
    groups = lax.axis_size("blk")
    bf16 = jnp.bfloat16
    anywhere = pl.BlockSpec(memory_space=pl.ANY)
    shard = pltpu.VMEM((rows, width), bf16)
    chunks = (CHUNKS, rows // PARTS, width // STRIPS)
    out = pl.pallas_call(
        functools.partial(kernel, groups),
        out_shape=pltpu.VMEM((rows, width), bf16),
        in_specs=[anywhere] * 6 + [pl.BlockSpec(memory_space=pltpu.SMEM)],
        out_specs=pl.BlockSpec(memory_space=pltpu.VMEM),
        scratch_shapes=[
            pltpu.VMEM((3, tokens, width), bf16),
            pltpu.VMEM((4, *chunks), bf16),
            shard,
            shard,
            shard,
            pltpu.VMEM((4, PARTS, rows // PARTS, tokens), bf16),
            pltpu.VMEM((2, rows // PARTS, tokens), jnp.float32),
            pltpu.VMEM((3, *chunks), bf16),
            pltpu.VMEM((5, *chunks), bf16),
            pltpu.VMEM(chunks, bf16),
            pltpu.VMEM(chunks, bf16),
            pltpu.VMEM(chunks, bf16),
            pltpu.SemaphoreType.DMA((6,)),
            pltpu.SemaphoreType.DMA((5, CHUNKS)),
            pltpu.SemaphoreType.DMA((4, CHUNKS)),
            pltpu.SemaphoreType.DMA((3, CHUNKS)),
            pltpu.SemaphoreType.DMA((5, CHUNKS)),
            pltpu.SemaphoreType.DMA((2, CHUNKS)),
            pltpu.SemaphoreType.DMA((2, CHUNKS)),
        ],
        compiler_params=pltpu.CompilerParams(collective_id=0, has_side_effects=True, vmem_limit_bytes=66306048),
    )(
        hidden[0],
        grad_query[0],
        grad_value[0],
        adapters[0],
        first_moment[0],
        second_moment[0],
        mixing,
    )
    return out[None]


def solution(mesh):
    spec = P("blk", "fsdp", None)
    in_specs = (spec,) * 6 + (P("blk", None),)
    body = fused if mesh.shape["fsdp"] == 4 and mesh.shape["blk"] > 2 else shards
    return jax.shard_map(body, mesh=mesh, in_specs=in_specs, out_specs=spec, check_vma=False)
```
